256 devices in a mesh: gx: 8 (over x, core), gy: 4 (over y), gz: 8 (over z).
Axes of the slice: x: 4, y: 4, z: 8, core: 2. Of those that a mesh axis runs over, the one named last changes fastest.
Arguments:
- ref_pos: float32 [8, 4, 8, 3, 20480], P('gx', 'gy', 'gz'), may hold values from -6 to 6
- step: float32 [8, 4, 8, 3, 20480], P('gx', 'gy', 'gz'), may hold values from -6 to 6
- inv_mass: float32 [8, 4, 8, 20480], P('gx', 'gy', 'gz'), may hold values from 0.08 to 1
- boundary: int32 [8, 4, 8, 1], P('gx', 'gy', 'gz'), may hold values from 0 to 18432, as said below
- bonds: int32 [8, 4, 8, 2, 24416], P('gx', 'gy', 'gz'), may hold values from 0 to 75775, as said below
Outputs:
- positions: float32 [8, 4, 8, 3, 20480], P('gx', 'gy', 'gz')
- max_deviation: float32 [3], replicated
The draws below stay inside these ranges and needn't reach their ends.
Inputs may be any that keep to these rules, and one draw needn't show every extreme that they name: Each domain's boundary atoms are the 2048 consecutive atoms from boundary on; boundary is a multiple of 2048. In each domain bond c * 127 + m, for the first 20320 bonds, joins atom 128 * c + m to atom 128 * c + m + 1 (chains of 128 consecutive atoms). Cross bond k (bond 20320 + k) joins the domain's boundary atom boundary + (k mod 2048) (first row) to entry k mod 2048 of one of the 26 neighbour blocks of the extended list (second row), never the centre block; which blocks are reached, and how many bonds each one receives, varies from domain to domain. Every such bond is also listed by that neighbour domain with its two ends swapped, the domain's atom then standing in the neighbour's opposite block.
All inputs are finite; a program needn't handle non-finite values.
Results may differ from the reference program's by a relative error of at most 0.00018.
Values sent between devices are 32-bit elements; how exact they have to be, the bound alone decides.
No kernel may reach another device: no remote copies, remote signals or barrier semaphores. Data moves between devices by JAX's collectives and lax.ppermute only.
A program may use at most 64 MiB of HBM per device.

```python
import math
import jax
import jax.numpy as jnp

ATOMS_DEV = 20480
BOUND = 2048
CROSS_BONDS = 4096
ITERS = 3
LOCAL_BONDS = 20320
N_GX = 8
N_GY = 4
N_GZ = 8


def draw_step(key, part):
    domains = N_GX * N_GY * N_GZ
    first_key, second_key = jax.random.split(key, 2)
    flat = jnp.arange(domains, dtype=jnp.float32).reshape(N_GX, N_GY, N_GZ, 1, 1) / max(domains - 1, 1)
    level = 0.1 * (1.0 + 2.0 * flat)
    factor = jnp.exp(jax.random.uniform(second_key, (N_GX, N_GY, N_GZ, 1, ATOMS_DEV), jnp.float32, jnp.log(0.5), jnp.log(2.0)))
    noise = jax.random.normal(first_key, (N_GX, N_GY, N_GZ, 3, ATOMS_DEV), jnp.float32)
    values = noise * level * factor
    return jnp.clip(values, -6.0, 6.0).astype(jnp.float32)


def boundary_start(key):
    runs = ATOMS_DEV // BOUND
    start = jax.random.randint(jax.random.fold_in(key, 11), (N_GX, N_GY, N_GZ, 1), 0, runs)
    return (start * BOUND).astype(jnp.int32)


def draw_boundary(key, part):
    return boundary_start(key)


def forced_phase(phase_now, coord, leaning):
    return jnp.where(leaning != 0, (coord + (leaning < 0).astype(jnp.int32)) % 2, phase_now).astype(jnp.int32)


def pair_number(coord, phase, extent):
    return ((coord - phase) % extent // 2).astype(jnp.int32)


def axis_moves(placed, switches, axis):
    swapped = jnp.take_along_axis(switches, (placed // 2).astype(jnp.int32), axis=axis)
    return (swapped * (1 - 2 * (placed % 2))).astype(jnp.int32)


def draw_bonds(key, part):
    grid = (N_GX, N_GY, N_GZ)
    domains = N_GX * N_GY * N_GZ
    start = boundary_start(key)
    chains = jnp.arange(ATOMS_DEV, dtype=jnp.int32).reshape(ATOMS_DEV // 128, 128)
    local_left = jnp.broadcast_to(chains[:, :-1].reshape(LOCAL_BONDS), grid + (LOCAL_BONDS,))
    local_right = jnp.broadcast_to(chains[:, 1:].reshape(LOCAL_BONDS), grid + (LOCAL_BONDS,))
    half = CROSS_BONDS // 2
    bond_rows = jnp.arange(half, dtype=jnp.int32)
    focus = jax.random.randint(jax.random.fold_in(key, 41), (), 0, domains).astype(jnp.int32)
    focus_x = focus // (N_GY * N_GZ)
    focus_y = focus // N_GZ % N_GY
    focus_z = focus % N_GZ
    chosen = jax.random.randint(jax.random.fold_in(key, 43), (), 0, 26).astype(jnp.int32)
    chosen = chosen + (chosen >= 13).astype(jnp.int32)
    lean_x = chosen // 9 - 1
    lean_y = chosen // 3 % 3 - 1
    lean_z = chosen % 3 - 1
    coord_z = jnp.arange(N_GZ, dtype=jnp.int32)
    phase_z = jax.random.randint(jax.random.fold_in(key, 47), (half,), 0, 2).astype(jnp.int32)
    phase_z = forced_phase(phase_z, focus_z, lean_z)
    switch_z = jax.random.randint(jax.random.fold_in(key, 53), (half, N_GZ // 2), 0, 2).astype(jnp.int32)
    switch_z = switch_z.at[bond_rows, pair_number(focus_z, phase_z, N_GZ)].set((lean_z != 0).astype(jnp.int32))
    placed_z = (coord_z[None, :] - phase_z[:, None]) % N_GZ
    offset_z = axis_moves(placed_z, switch_z, 1)
    coord_y = jnp.arange(N_GY, dtype=jnp.int32)
    phase_y = jax.random.randint(jax.random.fold_in(key, 59), (half, N_GZ), 0, 2).astype(jnp.int32)
    phase_y = phase_y.at[:, focus_z].set(forced_phase(phase_y[:, focus_z], focus_y, lean_y))
    switch_y = jax.random.randint(jax.random.fold_in(key, 61), (half, N_GZ, N_GY // 2), 0, 2).astype(jnp.int32)
    switch_y = switch_y.at[bond_rows, focus_z, pair_number(focus_y, phase_y[:, focus_z], N_GY)].set((lean_y != 0).astype(jnp.int32))
    placed_y = (coord_y[None, None, :] - phase_y[:, :, None]) % N_GY
    offset_y = axis_moves(placed_y, switch_y, 2)
    coord_x = jnp.arange(N_GX, dtype=jnp.int32)
    phase_x = jax.random.randint(jax.random.fold_in(key, 67), (half, N_GZ, N_GY), 0, 2).astype(jnp.int32)
    phase_x = phase_x.at[:, focus_z, focus_y].set(forced_phase(phase_x[:, focus_z, focus_y], focus_x, lean_x))
    switch_x = jax.random.randint(jax.random.fold_in(key, 71), (half, N_GZ, N_GY, N_GX // 2), 0, 2).astype(jnp.int32)
    standing = (offset_z[:, :, None] == 0) & (offset_y == 0)
    switch_x = jnp.where(standing[..., None], 1, switch_x).astype(jnp.int32)
    switch_x = switch_x.at[bond_rows, focus_z, focus_y, pair_number(focus_x, phase_x[:, focus_z, focus_y], N_GX)].set((lean_x != 0).astype(jnp.int32))
    placed_x = (coord_x[None, None, None, :] - phase_x[..., None]) % N_GX
    offset_x = axis_moves(placed_x, switch_x, 3)
    move_x = jnp.transpose(offset_x, (0, 3, 2, 1))
    move_y = jnp.transpose(offset_y, (0, 2, 1))[:, None, :, :]
    move_z = offset_z[:, None, None, :]
    first_block = (move_x + 1) * 9 + (move_y + 1) * 3 + (move_z + 1)
    first_block = jnp.broadcast_to(first_block, (half,) + grid).astype(jnp.int32)
    grid_x = coord_x[None, :, None, None]
    grid_y = coord_y[None, None, :, None]
    grid_z = coord_z[None, None, None, :]
    target = ((grid_x + move_x) % N_GX * N_GY + (grid_y + move_y) % N_GY) * N_GZ + (grid_z + move_z) % N_GZ
    target_flat = jnp.broadcast_to(target, (half,) + grid).reshape(half, domains).astype(jnp.int32)
    first_flat = first_block.reshape(half, domains)
    mirror_flat = jnp.zeros((half, domains), jnp.int32).at[bond_rows[:, None], target_flat].set(26 - first_flat)
    first_dom = jnp.transpose(first_flat.reshape((half,) + grid), (1, 2, 3, 0))
    mirror_dom = jnp.transpose(mirror_flat.reshape((half,) + grid), (1, 2, 3, 0))
    slot = bond_rows % BOUND
    own_left = jnp.broadcast_to(start + slot[None, None, None, :], grid + (half,))
    root_right = ATOMS_DEV + first_dom * BOUND + slot[None, None, None, :]
    mirror_right = ATOMS_DEV + mirror_dom * BOUND + slot[None, None, None, :]
    left_atom = jnp.concatenate([local_left, own_left, own_left], axis=3)
    right_atom = jnp.concatenate([local_right, root_right, mirror_right], axis=3)
    return jnp.stack([left_atom, right_atom], axis=3).astype(jnp.int32)


def levels(key, shape, cuts, low, high):
    factor_of, own = 1.0, jax.random.fold_in(key, 6)
    for position, shards_of in cuts:
        heights = jnp.exp(jax.random.uniform(jax.random.fold_in(own, position), (shards_of,), jnp.float32, low / len(cuts), high / len(cuts)))
        factor_of = factor_of * jnp.repeat(heights, shape[position] // shards_of).reshape([-1 if axis == position else 1 for axis in range(len(shape))])
    return factor_of


def centred(rng, dims, scale, most, pieces=(), kind=jnp.bfloat16):
    array = scale * jax.random.normal(rng, dims, jnp.float32)
    if pieces:
        array = array * levels(rng, dims, pieces, -0.22, 0.18)
    return jnp.clip(array, -most, most).astype(kind)


def setup_inputs(seed: int = 0) -> dict:
    key_list = jax.random.split(jax.random.key(seed), 6)
    ref_pos = centred(key_list[0], (N_GX, N_GY, N_GZ, 3, ATOMS_DEV), 1.0, 6.0, ((0, 8), (1, 4), (2, 8)), jnp.float32)
    step = draw_step(jax.random.fold_in(key_list[5], 71), 0)
    inv_mass = jnp.clip(jnp.exp(math.log(1.0) - 2.5257287 * jax.random.uniform(key_list[2], (N_GX, N_GY, N_GZ, ATOMS_DEV), jnp.float32) ** levels(key_list[2], (N_GX, N_GY, N_GZ, ATOMS_DEV), ((0, 8), (1, 4), (2, 8)), -0.2, 0.2)), 0.08, 1.0)
    boundary = draw_boundary(jax.random.fold_in(key_list[5], 71), 0)
    bonds = draw_bonds(jax.random.fold_in(key_list[5], 71), 0)
    return dict(ref_pos=ref_pos, step=step, inv_mass=inv_mass, boundary=boundary, bonds=bonds)


relax_factor = 0.7


def bond_terms(anchor_left, anchor_right, moved_left, moved_right, inverse_left, inverse_right):
    bond_rest = anchor_left - anchor_right
    bond_now = moved_left - moved_right
    rest_sq = jnp.sum(bond_rest * bond_rest, axis=0)
    now_sq = jnp.sum(bond_now * bond_now, axis=0)
    inner = jnp.sum(bond_rest * bond_now, axis=0)
    excess = now_sq - rest_sq
    deviation = jnp.max(jnp.abs(excess) / (2.0 * jnp.maximum(rest_sq, 1.0)))
    factor = relax_factor * excess / (2.0 * (inverse_left + inverse_right) * jnp.maximum(inner, 1.0))
    return factor * bond_rest, deviation


def apply_terms(current, shift_term, left_atom, right_atom, inverse_left, inverse_right):
    current = current.at[:, left_atom].add(-shift_term * inverse_left, mode="drop")
    return current.at[:, right_atom].add(shift_term * inverse_right, mode="drop")


def neighbours(rims):
    blocks = []
    for first_off in (-1, 0, 1):
        for second_off in (-1, 0, 1):
            for third_off in (-1, 0, 1):
                blocks.append(jnp.roll(rims, (-first_off, -second_off, -third_off), axis=(0, 1, 2)))
    return jnp.concatenate(blocks, axis=4)


def sweep(anchor_ext, inverse_ext, moved_ext, bond_pairs):
    left_atom = bond_pairs[0]
    right_atom = bond_pairs[1]
    inverse_left = inverse_ext[left_atom]
    inverse_right = inverse_ext[right_atom]
    shift_term, deviation = bond_terms(anchor_ext[:, left_atom], anchor_ext[:, right_atom],
                                       moved_ext[:, left_atom], moved_ext[:, right_atom],
                                       inverse_left, inverse_right)
    atoms = moved_ext.shape[1] - 27 * BOUND
    owned = moved_ext[:, :atoms]
    return apply_terms(owned, shift_term, left_atom, right_atom, inverse_left, inverse_right), deviation


def reference(ref_pos, step, inv_mass, boundary, bonds):
    edge_rows = (boundary + jnp.arange(BOUND, dtype=jnp.int32)[None, None, None, :]).astype(jnp.int32)

    def extend(values_in):
        picker = jnp.broadcast_to(edge_rows[:, :, :, None, :],
                                  values_in.shape[:4] + (BOUND,))
        rims = jnp.take_along_axis(values_in, picker, axis=4)
        whole = jnp.concatenate([values_in, neighbours(rims)], axis=4)
        return whole.reshape((-1,) + whole.shape[3:])

    anchor_ext = extend(ref_pos)
    inverse_ext = extend(inv_mass[:, :, :, None, :])[:, 0]
    bond_flat = bonds.reshape((-1,) + bonds.shape[3:])
    current = ref_pos + step
    reports = []
    for iteration in range(ITERS):
        moved_ext = extend(current)
        updated, deviation = jax.vmap(sweep)(anchor_ext, inverse_ext, moved_ext, bond_flat)
        current = updated.reshape(current.shape)
        reports.append(jnp.max(deviation))
    return current, jnp.stack(reports).astype(jnp.float32)
```

```python
import jax
import jax.numpy as jnp
from jax import lax
from jax.sharding import PartitionSpec as P

ATOMS_DEV = 20480
BOUND = 2048
CROSS_BONDS = 4096
ITERS = 3
LOCAL_BONDS = 20320
LANES = 128
CHAINS = ATOMS_DEV // LANES
RIM_CHAINS = BOUND // LANES
GROUPS = CROSS_BONDS // BOUND
AXES = ("gx", "gy", "gz")
WEIGHT = {"gx": 9, "gy": 3, "gz": 1}
ORDER = ("gx", "gy", "gz")

relax_factor = 0.7


def partners(count):
    first = [(i, i ^ 1) for i in range(count)]
    second = [(i, (i + 1) % count if i % 2 else (i - 1) % count) for i in range(count)]
    return first, second


def swap_both(first_send, second_send, axis):
    first, second = partners(lax.axis_size(axis))
    return lax.ppermute(first_send, axis, first), lax.ppermute(second_send, axis, second)


def dot(left, right):
    return left[0] * right[0] + left[1] * right[1] + left[2] * right[2]


def bond_numbers(rest, rest_sq, now, inverse_sum):
    excess = dot(now, now) - rest_sq
    deviation = jnp.abs(excess) / (2.0 * jnp.maximum(rest_sq, 1.0))
    factor = relax_factor * excess / (2.0 * inverse_sum * jnp.maximum(dot(rest, now), 1.0))
    return factor, deviation


def next_atom(values):
    return jnp.roll(values, -1, axis=-1)


def chain_step(anchor, inverse, current):
    lane = lax.broadcasted_iota(jnp.int32, inverse.shape, 1)
    inside = lane < LANES - 1
    rest = [a - next_atom(a) for a in anchor]
    now = [c - next_atom(c) for c in current]
    factor, deviation = bond_numbers(rest, dot(rest, rest), now, inverse + next_atom(inverse))
    factor = jnp.where(inside, factor, 0.0)
    terms = [factor * r for r in rest]
    delta = [(jnp.roll(t, 1, axis=-1) - t) * inverse for t in terms]
    return delta, jnp.where(inside, deviation, 0.0)


def pick(blocks, index):
    picked = blocks[0]
    for number in range(1, 9):
        picked = jnp.where(index == number, blocks[number], picked)
    return picked


def local(ref_pos, step, inv_mass, boundary, bonds):
    anchor = ref_pos[0, 0, 0].reshape(3, CHAINS, LANES)
    moved = anchor + step[0, 0, 0].reshape(3, CHAINS, LANES)
    inverse = inv_mass[0, 0, 0].reshape(CHAINS, LANES)
    first_chain = boundary[0, 0, 0, 0] // LANES

    def rim(values):
        return lax.dynamic_slice_in_dim(values, first_chain, RIM_CHAINS, values.ndim - 2)

    sign = {a: 1 - 2 * (lax.axis_index(a) % 2) for a in AXES}
    offsets = {a: (sign[a], 0, -sign[a]) for a in AXES}
    ids = ((bonds[0, 0, 0, 1, LOCAL_BONDS:] - ATOMS_DEV) // BOUND).reshape(GROUPS, RIM_CHAINS, LANES)
    parts = {"gx": ids // 9 - 1, "gy": ids // 3 % 3 - 1, "gz": ids % 3 - 1}
    place = {a: 1 - parts[a] * sign[a] for a in AXES}
    s0, s1, s2 = ORDER
    spot = place[s1] * 3 + place[s0]
    plane = place[s2]
    both = plane[0] == plane[1]
    use_last = jnp.stack([both & (spot[1] < spot[0]), both & (spot[0] < spot[1])])

    rim_anchor = rim(anchor)
    rim_inverse = rim(inverse)
    rim_moved = rim(moved)

    def columns(values):
        one, two = swap_both(values, values, s0)
        row = jnp.stack([one, values, two])
        one, two = swap_both(row, row, s1)
        return [b[i] for b in (one, row, two) for i in range(3)]

    def gather(blocks, tables):
        first_send = jnp.stack([pick(blocks, tables[0][0]), pick(blocks, tables[0][1])])
        second_send = jnp.stack([pick(blocks, tables[1][0]), pick(blocks, tables[1][1])])
        one, two = swap_both(first_send, second_send, s2)
        far = []
        for group in range(GROUPS):
            last = use_last[group]
            here = pick(blocks, spot[group])
            from_one = jnp.where(last, one[1], one[0])
            from_two = jnp.where(last, two[1], two[0])
            far.append(
                jnp.where(plane[group] == 1, here, jnp.where(plane[group] == 0, from_one, from_two))
            )
        return far

    payload = jnp.concatenate(
        [rim_anchor, rim_moved, rim_inverse[None], ids.astype(jnp.float32)], axis=0
    )
    blocks = columns(payload)

    def wanted(toward):
        first_spot = jnp.full((RIM_CHAINS, LANES), 9, jnp.int32)
        last_spot = jnp.full((RIM_CHAINS, LANES), -1, jnp.int32)
        for number in range(9):
            back0 = offsets[s0][number % 3]
            back1 = offsets[s1][number // 3]
            code = 13 - back0 * WEIGHT[s0] - back1 * WEIGHT[s1] + toward * WEIGHT[s2]
            code = jnp.asarray(code, jnp.float32)
            found = (blocks[number][7] == code) | (blocks[number][8] == code)
            first_spot = jnp.minimum(first_spot, jnp.where(found, number, 9))
            last_spot = jnp.maximum(last_spot, jnp.where(found, number, -1))
        return first_spot, last_spot

    tables = (wanted(offsets[s2][0]), wanted(offsets[s2][2]))
    far = gather([b[:7] for b in blocks], tables)
    cross_rest = [[rim_anchor[i] - far[g][i] for i in range(3)] for g in range(GROUPS)]
    cross_sq = [dot(cross_rest[g], cross_rest[g]) for g in range(GROUPS)]
    cross_inverse = [rim_inverse + far[g][6] for g in range(GROUPS)]
    far_moved = [far[g][3:6] for g in range(GROUPS)]

    chain = lax.broadcasted_iota(jnp.int32, (CHAINS, LANES), 0)
    outside = (chain < first_chain) | (chain >= first_chain + RIM_CHAINS)
    body = [moved[i] for i in range(3)]
    edge = [rim_moved[i] for i in range(3)]
    reports = []
    for iteration in range(ITERS):
        delta, deviation = chain_step([anchor[i] for i in range(3)], inverse, body)
        body = [b + d for b, d in zip(body, delta)]
        body_worst = jnp.max(jnp.where(outside, deviation, 0.0))

        if iteration > 0:
            far_moved = gather(columns(jnp.stack(edge)), tables)
        delta, rim_dev = chain_step([rim_anchor[i] for i in range(3)], rim_inverse, edge)
        shift = [jnp.zeros((RIM_CHAINS, LANES), jnp.float32)] * 3
        for group in range(GROUPS):
            now = [edge[i] - far_moved[group][i] for i in range(3)]
            factor, deviation = bond_numbers(
                cross_rest[group], cross_sq[group], now, cross_inverse[group]
            )
            shift = [s + factor * r for s, r in zip(shift, cross_rest[group])]
            rim_dev = jnp.maximum(rim_dev, deviation)
        edge = [e + d - s * rim_inverse for e, d, s in zip(edge, delta, shift)]
        reports.append(jnp.maximum(body_worst, jnp.max(rim_dev)))

    positions = lax.dynamic_update_slice_in_dim(jnp.stack(body), jnp.stack(edge), first_chain, 1)

    devices = 1
    for a in AXES:
        devices *= lax.axis_size(a)
    lane = lax.broadcasted_iota(jnp.int32, (devices, LANES), 1)
    row = jnp.where(lane == 0, reports[0], jnp.where(lane == 1, reports[1], reports[2]))
    seen = lax.all_to_all(row, AXES, 0, 0, tiled=True)
    summary = jnp.max(seen, axis=0)[:ITERS]
    return positions.reshape(1, 1, 1, 3, ATOMS_DEV), summary


def solution(mesh):
    placed = (
        P("gx", "gy", "gz", None, None),
        P("gx", "gy", "gz", None, None),
        P("gx", "gy", "gz", None),
        P("gx", "gy", "gz", None),
        P("gx", "gy", "gz", None, None),
    )
    return jax.shard_map(
        local,
        mesh=mesh,
        in_specs=placed,
        out_specs=(P("gx", "gy", "gz", None, None), P()),
        check_vma=False,
    )
```

```python
import jax
import jax.numpy as jnp
from jax import lax
from jax.experimental import pallas as pl
from jax.experimental.pallas import tpu as pltpu
from jax.sharding import PartitionSpec as P

ATOMS_DEV = 20480
BOUND = 2048
CROSS_BONDS = 4096
ITERS = 3
LOCAL_BONDS = 20320
LANES = 128
CHAINS = ATOMS_DEV // LANES
RIM_CHAINS = BOUND // LANES
GROUPS = CROSS_BONDS // BOUND
AXES = ("gx", "gy", "gz")
WEIGHT = {"gx": 9, "gy": 3, "gz": 1}
ORDER = ("gy", "gx", "gz")
SHIFTED = ("gy", "gz", )

relax_factor = 0.7


def partners(count):
    first = [(i, i ^ 1) for i in range(count)]
    second = [(i, (i + 1) % count if i % 2 else (i - 1) % count) for i in range(count)]
    return first, second


def swap_both(first_send, second_send, axis):
    count = lax.axis_size(axis)
    if axis in SHIFTED:
        first = [(i, (i + 1) % count) for i in range(count)]
        second = [((i + 1) % count, i) for i in range(count)]
    else:
        first, second = partners(count)
    return lax.ppermute(first_send, axis, first), lax.ppermute(second_send, axis, second)


def dot(left, right):
    return left[0] * right[0] + left[1] * right[1] + left[2] * right[2]


def bond_numbers(rest, rest_sq, now, inverse_sum):
    excess = dot(now, now) - rest_sq
    deviation = jnp.abs(excess) / (2.0 * jnp.maximum(rest_sq, 1.0))
    factor = relax_factor * excess / (2.0 * inverse_sum * jnp.maximum(dot(rest, now), 1.0))
    return factor, deviation


def near(values):
    return pltpu.with_memory_space_constraint(values, pltpu.VMEM)


def next_atom(values):
    return pltpu.roll(values, LANES - 1, 1)


def chain_shift(factor, rest, inverse):
    terms = [factor * r for r in rest]
    return [(pltpu.roll(t, 1, 1) - t) * inverse for t in terms]


def fold(values):
    return jnp.maximum(values[:8], values[8:])


def body_kernel(place_ref, anchor_ref, step_ref, inverse_ref, out_ref, worst_ref):
    inside = lax.broadcasted_iota(jnp.int32, (8, LANES), 1) < LANES - 1
    rim_block = place_ref[0] * (RIM_CHAINS // 8)

    def block(number, worst):
        rows = pl.ds(pl.multiple_of(number * 8, 8), 8)
        anchor = [anchor_ref[i, rows, :] for i in range(3)]
        current = [anchor[i] + step_ref[i, rows, :] for i in range(3)]
        inverse = inverse_ref[rows, :]
        counted = (number < rim_block) | (number >= rim_block + RIM_CHAINS // 8)
        rest = [a - next_atom(a) for a in anchor]
        rest_sq = dot(rest, rest)
        inverse_sum = inverse + next_atom(inverse)
        found = []
        for iteration in range(ITERS):
            now = [c - next_atom(c) for c in current]
            factor, deviation = bond_numbers(rest, rest_sq, now, inverse_sum)
            factor = jnp.where(inside, factor, 0.0)
            delta = chain_shift(factor, rest, inverse)
            current = [c + d for c, d in zip(current, delta)]
            found.append(jnp.maximum(worst[iteration], jnp.where(inside & counted, deviation, 0.0)))
        for i in range(3):
            out_ref[i, rows, :] = current[i]
        return tuple(found)

    zero = jnp.zeros((8, LANES), jnp.float32)
    worst = lax.fori_loop(0, CHAINS // 8, block, (zero,) * ITERS, unroll=4)
    for iteration in range(ITERS):
        worst_ref[iteration] = worst[iteration]


def run_body(place, anchor, step, inverse):
    smem = pl.BlockSpec(memory_space=pltpu.SMEM)
    vmem = pl.BlockSpec(memory_space=pltpu.VMEM)
    return pl.pallas_call(
        body_kernel,
        in_specs=[smem, vmem, vmem, vmem],
        out_specs=[vmem, vmem],
        out_shape=[
            pltpu.VMEM((3, CHAINS, LANES), jnp.float32),
            pltpu.VMEM((ITERS, 8, LANES), jnp.float32),
        ],
        cost_estimate=pl.CostEstimate(flops=6000000, transcendentals=0, bytes_accessed=900000),
        name="body",
    )(place, near(anchor), near(step), near(inverse))


def load_kernel(place_ref, anchor_ref, step_ref, inverse_ref, bonds_ref, out_ref, rows_ref):
    start = LOCAL_BONDS // LANES * LANES
    tail = LOCAL_BONDS - start
    rows = CROSS_BONDS // LANES
    for row in range(rows):
        rows_ref[row : row + 1, :] = bonds_ref[1:2, start + row * LANES : start + (row + 1) * LANES]
    rows_ref[rows : rows + 1, :tail] = bonds_ref[1:2, start + rows * LANES :]
    head = pltpu.roll(rows_ref[:rows, :], LANES - tail, 1)
    rest = pltpu.roll(rows_ref[1 : rows + 1, :], LANES - tail, 1)
    lane = lax.broadcasted_iota(jnp.int32, (rows, LANES), 1)
    ids = ((jnp.where(lane < LANES - tail, head, rest) - ATOMS_DEV) // BOUND).astype(jnp.float32)
    for i in range(3):
        out_ref[i] = anchor_ref[i]
        out_ref[3 + i] = anchor_ref[i] + step_ref[i]
    out_ref[6] = inverse_ref[...]
    for group in range(GROUPS):
        out_ref[7 + group] = ids[group * RIM_CHAINS : (group + 1) * RIM_CHAINS]


def run_load(place, anchor, step, inverse, bonds):
    rim3 = pl.BlockSpec((3, RIM_CHAINS, LANES), lambda i, place: (0, place[0], 0))
    rim1 = pl.BlockSpec((RIM_CHAINS, LANES), lambda i, place: (place[0], 0))
    whole = pl.BlockSpec(bonds.shape, lambda i, place: (0, 0))
    return pl.pallas_call(
        load_kernel,
        grid_spec=pltpu.PrefetchScalarGridSpec(
            num_scalar_prefetch=1,
            grid=(1,),
            in_specs=[rim3, rim3, rim1, whole],
            out_specs=pl.BlockSpec((9, RIM_CHAINS, LANES), lambda i, place: (0, 0, 0)),
            scratch_shapes=[pltpu.VMEM((CROSS_BONDS // LANES + 8, LANES), jnp.int32)],
        ),
        out_shape=pltpu.VMEM((9, RIM_CHAINS, LANES), jnp.float32),
        name="load",
    )(place, anchor, step, inverse, bonds)


def peak_kernel(seen_ref, out_ref):
    out_ref[...] = jnp.max(seen_ref[...], axis=0, keepdims=True)


def run_peak(seen):
    vmem = pl.BlockSpec(memory_space=pltpu.VMEM)
    return pl.pallas_call(
        peak_kernel,
        in_specs=[vmem],
        out_specs=vmem,
        out_shape=pltpu.VMEM((1, LANES), jnp.float32),
        name="peak",
    )(near(seen))


def edge_kernel(first, last, *refs):
    refs = list(refs)
    payload_ref = refs.pop(0)
    edge_ref = payload_ref if first else refs.pop(0)
    static_ref = None if first else refs.pop(0)
    one_ref, two_ref, here_ref, source_ref = [refs.pop(0) for _ in range(4)]
    lane = lax.broadcasted_iota(jnp.int32, (RIM_CHAINS, LANES), 1)
    inside = lane < LANES - 1
    anchor = [payload_ref[i] for i in range(3)]
    inverse = payload_ref[6]
    edge = [edge_ref[3 + i] if first else edge_ref[i] for i in range(3)]
    rest = [a - next_atom(a) for a in anchor]
    now = [c - next_atom(c) for c in edge]
    factor, deviation = bond_numbers(rest, dot(rest, rest), now, inverse + next_atom(inverse))
    delta = chain_shift(jnp.where(inside, factor, 0.0), rest, inverse)
    worst = jnp.where(inside, deviation, 0.0)
    shift = [0.0, 0.0, 0.0]
    kept = []
    for group in range(GROUPS):
        source = source_ref[group]

        def far(field):
            return jnp.where(
                source < 2,
                jnp.where(source == 0, one_ref[0, field], one_ref[1, field]),
                jnp.where(
                    source == 4,
                    here_ref[group, field],
                    jnp.where(source == 2, two_ref[0, field], two_ref[1, field]),
                ),
            )

        if first:
            far_anchor = [far(i) for i in range(3)]
            far_moved = [far(3 + i) for i in range(3)]
            far_inverse = far(6)
            kept.append(far_anchor + [far_inverse])
        else:
            far_anchor = [static_ref[group, i] for i in range(3)]
            far_inverse = static_ref[group, 3]
            far_moved = [far(i) for i in range(3)]
        rest = [a - f for a, f in zip(anchor, far_anchor)]
        now = [c - f for c, f in zip(edge, far_moved)]
        factor, deviation = bond_numbers(rest, dot(rest, rest), now, inverse + far_inverse)
        shift = [s + factor * r for s, r in zip(shift, rest)]
        worst = jnp.maximum(worst, deviation)
    edge = [e + d - s * inverse for e, d, s in zip(edge, delta, shift)]
    if last:
        worst_body_ref, worst0_ref, worst1_ref, out_ref, row_ref = refs
        found = []
        for iteration, rim in enumerate((worst0_ref[...], worst1_ref[...], fold(worst))):
            found.append(jnp.max(jnp.maximum(worst_body_ref[iteration], rim)))
        lane = lax.broadcasted_iota(jnp.int32, row_ref.shape, 1)
        row_ref[...] = jnp.where(lane == 0, found[0], jnp.where(lane == 1, found[1], found[2]))
    elif first:
        out_ref, worst_ref, kept_ref = refs
        worst_ref[...] = fold(worst)
        for group in range(GROUPS):
            for field in range(4):
                kept_ref[group, field] = kept[group][field]
    else:
        out_ref, worst_ref = refs
        worst_ref[...] = fold(worst)
    for i in range(3):
        out_ref[i] = edge[i]


def run_edge(first, last, devices, *operands):
    vmem = pl.BlockSpec(memory_space=pltpu.VMEM)
    shapes = [(3, RIM_CHAINS, LANES)]
    shapes.append((devices, LANES) if last else (8, LANES))
    if first:
        shapes.append((GROUPS, 4, RIM_CHAINS, LANES))
    return pl.pallas_call(
        lambda *refs: edge_kernel(first, last, *refs),
        in_specs=[vmem] * len(operands),
        out_specs=[vmem] * len(shapes),
        out_shape=[pltpu.VMEM(s, jnp.float32) for s in shapes],
        name="edge",
    )(*[near(operand) for operand in operands])


def pick(blocks, index):
    picked = blocks[0]
    for number in range(1, 9):
        picked = jnp.where(index == number, blocks[number], picked)
    return picked


def local(ref_pos, step, inv_mass, boundary, bonds):
    anchor = ref_pos.reshape(3, CHAINS, LANES)
    step = step.reshape(3, CHAINS, LANES)
    inverse = inv_mass.reshape(CHAINS, LANES)
    place_rim = (boundary // BOUND).reshape(1)

    sign = {a: -1 if a in SHIFTED else 1 - 2 * (lax.axis_index(a) % 2) for a in AXES}
    offsets = {a: (sign[a], 0, -sign[a]) for a in AXES}
    payload = run_load(place_rim, anchor, step, inverse, bonds[0, 0, 0])
    ids = payload[7:].astype(jnp.int32)
    parts = {"gx": ids // 9 - 1, "gy": ids // 3 % 3 - 1, "gz": ids % 3 - 1}
    place = {a: 1 - parts[a] * sign[a] for a in AXES}
    s0, s1, s2 = ORDER
    spot = place[s1] * 3 + place[s0]
    plane = place[s2]
    both = plane[0] == plane[1]
    use_last = jnp.stack([both & (spot[1] < spot[0]), both & (spot[0] < spot[1])]).astype(jnp.int32)
    source = jnp.where(plane == 1, 4, plane + use_last)

    def columns(values):
        one, two = swap_both(values, values, s0)
        row = jnp.stack([one, values, two])
        one, two = swap_both(row, row, s1)
        return [b[i] for b in (one, row, two) for i in range(3)]

    def exchange(blocks, tables):
        first_send = jnp.stack([pick(blocks, tables[0][0]), pick(blocks, tables[0][1])])
        second_send = jnp.stack([pick(blocks, tables[1][0]), pick(blocks, tables[1][1])])
        one, two = swap_both(first_send, second_send, s2)
        return one, two, jnp.stack([pick(blocks, spot[0]), pick(blocks, spot[1])])

    blocks = columns(payload)

    def wanted(toward):
        first_spot = jnp.full((RIM_CHAINS, LANES), 9, jnp.int32)
        last_spot = jnp.full((RIM_CHAINS, LANES), -1, jnp.int32)
        for number in range(9):
            back0 = offsets[s0][number % 3]
            back1 = offsets[s1][number // 3]
            code = 13 - back0 * WEIGHT[s0] - back1 * WEIGHT[s1] + toward * WEIGHT[s2]
            code = jnp.asarray(code, jnp.float32)
            found = (blocks[number][7] == code) | (blocks[number][8] == code)
            first_spot = jnp.minimum(first_spot, jnp.where(found, number, 9))
            last_spot = jnp.maximum(last_spot, jnp.where(found, number, -1))
        return first_spot, last_spot

    turn = -1 if s2 in SHIFTED else 1
    tables = (wanted(turn * offsets[s2][0]), wanted(turn * offsets[s2][2]))
    body, worst_body = run_body(place_rim, anchor, step, inverse)
    devices = 1
    for a in AXES:
        devices *= lax.axis_size(a)

    one, two, here = exchange([b[:7] for b in blocks], tables)
    edge, worst0, kept = run_edge(True, False, devices, payload, one, two, here, source)
    one, two, here = exchange(columns(edge), tables)
    edge, worst1 = run_edge(False, False, devices, payload, edge, kept, one, two, here, source)
    one, two, here = exchange(columns(edge), tables)
    edge, row = run_edge(
        False, True, devices, payload, edge, kept, one, two, here, source, worst_body, worst0, worst1
    )
    seen = lax.all_to_all(row, AXES, 0, 0, tiled=True)
    positions = lax.dynamic_update_slice_in_dim(body, edge, place_rim[0] * RIM_CHAINS, 1)
    summary = run_peak(seen)[0, :ITERS]
    return positions.reshape(1, 1, 1, 3, ATOMS_DEV), summary


def solution(mesh):
    placed = (
        P("gx", "gy", "gz", None, None),
        P("gx", "gy", "gz", None, None),
        P("gx", "gy", "gz", None),
        P("gx", "gy", "gz", None),
        P("gx", "gy", "gz", None, None),
    )
    return jax.shard_map(
        local,
        mesh=mesh,
        in_specs=placed,
        out_specs=(P("gx", "gy", "gz", None, None), P()),
        check_vma=False,
    )
```
